32 devices in a mesh: dp: 4 (over y, x), expert: 8 (over z, core).
Axes of the slice: x: 2, y: 2, z: 4, core: 2. Of those that a mesh axis runs over, the one named last changes fastest.
Arguments:
- tokens: bfloat16 [4096, 7168], P(('dp', 'expert')), may hold values from -6 to 6
- route_ids: int32 [4096, 8], P(('dp', 'expert')), may hold values from 0 to 255, as said below
- gate_weights: float32 [4096, 8], P(('dp', 'expert')), may hold values from 0.3 to 1.2
- gate_weight: bfloat16 [8, 7168, 1024], P('expert', 'dp'), may hold values from -0.0625 to 0.0625
- up_weight: bfloat16 [8, 7168, 1024], P('expert', 'dp'), may hold values from -0.0625 to 0.0625
- down_weight: bfloat16 [8, 7168, 1024], P('expert', 'dp'), may hold values from -0.1875 to 0.1875
- cotangent: bfloat16 [4096, 7168], P(('dp', 'expert')), may hold values from -3 to 3
Outputs:
- output: bfloat16 [4096, 7168], P(('dp', 'expert'))
- grad_tokens: bfloat16 [4096, 7168], P(('dp', 'expert'))
- grad_gate: bfloat16 [8, 7168, 1024], P('expert', 'dp')
- grad_up: bfloat16 [8, 7168, 1024], P('expert', 'dp')
- grad_down: bfloat16 [8, 7168, 1024], P('expert', 'dp')
The draws below stay inside these ranges and needn't reach their ends.
Inputs may be any that keep to these rules, and one draw needn't show every extreme that they name: `route_ids`: each token's 8 numbers are different, and at most one of them is below 8. Among the 128 tokens of one device at most 4 name any one number below 8; for each index of dp, one number below 8 is named by exactly 4 tokens of every device with that index.
All inputs are finite; a program needn't handle non-finite values.
Results may differ from the reference program's by a relative error of at most 0.018.
Values may be sent and summed in bfloat16 or wider, within the bound.
No kernel may reach another device: no remote copies, remote signals or barrier semaphores. Data moves between devices by JAX's collectives and lax.ppermute only.
A program may use at most 128 MiB of HBM per device.

```python
import jax
import jax.numpy as jnp
from jax import lax

D = 7168
FF = 1024
ROUTED = 256
TOP = 8
CAP = 4
TOK_DEV = 128
EXPERTS = 8
TOKENS = 4096
N_DP = 4


def draw_route_ids(key, part):
    blocks = TOKENS // TOK_DEV
    groups = blocks // EXPERTS
    keys = jax.random.split(key, 6)
    heavy_pick = jax.random.randint(keys[0], (groups,), 0, EXPERTS)
    heavy_block = jnp.repeat(heavy_pick, EXPERTS)
    heavy = jnp.arange(EXPERTS)[None, :] == heavy_block[:, None]
    light = jax.random.randint(keys[1], (blocks, EXPERTS), 1, CAP + 1)
    counts = jnp.where(heavy, CAP, light)
    shuffled = jax.vmap(lambda subkey: jax.random.permutation(subkey, TOK_DEV))(jax.random.split(keys[3], blocks))
    target = shuffled // CAP
    within = shuffled % CAP
    bounded = jnp.minimum(target, EXPERTS - 1)
    limit = jnp.take_along_axis(counts, bounded, axis=1)
    live = (target < EXPERTS) & (within < limit)
    spread = ROUTED - EXPERTS
    stride = spread // TOP
    offsets = jax.random.randint(keys[4], (blocks, TOK_DEV), 0, spread)
    outside = EXPERTS + (offsets[:, :, None] + stride * jnp.arange(TOP)[None, None, :]) % spread
    column = jax.random.randint(keys[5], (blocks, TOK_DEV), 0, TOP)
    chosen = live[:, :, None] & (jnp.arange(TOP)[None, None, :] == column[:, :, None])
    table = jnp.where(chosen, target[:, :, None], outside)
    return table.reshape(TOKENS, TOP).astype(jnp.int32)


def block_levels(own_key, extent, cuts, least, largest):
    def one(dim, blocks):
        heights = jax.random.uniform(jax.random.fold_in(jax.random.fold_in(own_key, 6), dim), (blocks,), jnp.float32, least / len(cuts), largest / len(cuts))
        return jnp.repeat(jnp.exp(heights), extent[dim] // blocks).reshape((-1,) + (1,) * (len(extent) - dim - 1))

    loudness = one(*cuts[0])
    for cut in cuts[1:]:
        loudness = loudness * one(*cut)
    return loudness


def gaussian(stream_key, shape, scale, reach, cuts=(), held_as=jnp.bfloat16):
    result = jax.random.normal(stream_key, shape, jnp.float32) * scale
    if len(cuts) > 0:
        result = block_levels(stream_key, shape, cuts, -0.22, 0.18) * result
    return jnp.clip(result, min=-reach, max=reach).astype(held_as)


def setup_inputs(seed: int = 0) -> dict:
    streams_of = jax.random.split(jax.random.key(seed), 8)
    return {
        "tokens": gaussian(streams_of[0], (TOKENS, D), 1.0, 6.0, ((0, 32),)),
        "route_ids": draw_route_ids(jax.random.fold_in(streams_of[7], 71), 0),
        "gate_weights": jnp.clip(0.3 + 0.90000004 * jax.random.uniform(streams_of[2], (TOKENS, TOP), jnp.float32) ** block_levels(streams_of[2], (TOKENS, TOP), ((0, 32),), -0.2, 0.2), 0.3, 1.2),
        "gate_weight": gaussian(streams_of[3], (EXPERTS, D, FF), D ** -0.5, 0.0625, ((0, 8), (1, 4))),
        "up_weight": gaussian(streams_of[4], (EXPERTS, D, FF), D ** -0.5, 0.0625, ((0, 8), (1, 4))),
        "down_weight": gaussian(streams_of[5], (EXPERTS, D, FF), FF ** -0.5, 0.1875, ((0, 8), (1, 4))),
        "cotangent": gaussian(streams_of[6], (TOKENS, D), 0.5, 3.0, ((0, 32),)),
    }


def split_sum(rows, weight):
    count = rows.shape[0]
    pieces = rows.reshape(count, N_DP, D // N_DP).astype(jnp.float32)
    blocks = weight.reshape(N_DP, D // N_DP, FF).astype(jnp.float32)
    terms = jnp.einsum("rpd,pdf->prf", pieces, blocks)
    rounded = lax.optimization_barrier(terms.astype(jnp.bfloat16))
    return jnp.sum(rounded.astype(jnp.float32), axis=0)


def expert_pass(operands):
    rows, grads, gate_mat, up_mat, down_mat = operands
    pre_gate = split_sum(rows, gate_mat)
    pre_up = split_sum(rows, up_mat)
    hidden_grad = split_sum(grads, down_mat)
    squash = jax.nn.sigmoid(pre_gate)
    silu_gate = pre_gate * squash
    hidden = (silu_gate * pre_up).astype(jnp.bfloat16)
    gate_grad = (hidden_grad * pre_up * squash * (1.0 + pre_gate * (1.0 - squash))).astype(jnp.bfloat16)
    up_grad = (hidden_grad * silu_gate).astype(jnp.bfloat16)
    expert_out = jnp.dot(hidden, down_mat.T, preferred_element_type=jnp.float32).astype(jnp.bfloat16)
    row_grad = (jnp.dot(gate_grad, gate_mat.T, preferred_element_type=jnp.float32)
                + jnp.dot(up_grad, up_mat.T, preferred_element_type=jnp.float32)).astype(jnp.bfloat16)
    gate_total = jnp.dot(rows.T, gate_grad, preferred_element_type=jnp.float32).astype(jnp.bfloat16)
    up_total = jnp.dot(rows.T, up_grad, preferred_element_type=jnp.float32).astype(jnp.bfloat16)
    down_total = jnp.dot(grads.T, hidden, preferred_element_type=jnp.float32).astype(jnp.bfloat16)
    return expert_out, row_grad, gate_total, up_total, down_total


def reference(tokens, route_ids, gate_weights, gate_weight, up_weight, down_weight, cotangent):
    blocks = TOKENS // TOK_DEV
    labels = jnp.arange(EXPERTS, dtype=jnp.int32)
    table = route_ids.reshape(blocks, TOK_DEV, TOP)
    weights = gate_weights.reshape(blocks, TOK_DEV, TOP)
    matches = table[:, :, :, None] == labels
    chosen = jnp.any(matches, axis=2).astype(jnp.int32)
    gate_of = jnp.sum(jnp.where(matches, weights[:, :, :, None], 0.0), axis=2)
    ranks = jnp.cumsum(chosen, axis=1) - chosen
    placed = (chosen[:, :, :, None] == 1) & (ranks[:, :, :, None] == jnp.arange(CAP, dtype=jnp.int32))
    positions = jnp.arange(TOK_DEV, dtype=jnp.int32)[None, :, None, None]
    local_index = jnp.sum(jnp.where(placed, positions, 0), axis=1).astype(jnp.int32)
    slot_gate = jnp.sum(jnp.where(placed, gate_of[:, :, :, None], 0.0), axis=1)
    alive_slots = jnp.any(placed, axis=1)
    token_index = (local_index + TOK_DEV * jnp.arange(blocks, dtype=jnp.int32)[:, None, None]).astype(jnp.int32)
    order = jnp.transpose(token_index, (1, 0, 2)).reshape(EXPERTS, blocks * CAP)
    alive = jnp.transpose(alive_slots, (1, 0, 2)).reshape(EXPERTS, blocks * CAP)
    gains = jnp.transpose(slot_gate, (1, 0, 2)).reshape(EXPERTS, blocks * CAP)
    rows = jnp.where(alive[:, :, None], tokens[order], jnp.zeros((), jnp.bfloat16))
    grads = (gains[:, :, None] * cotangent[order].astype(jnp.float32)).astype(jnp.bfloat16)
    expert_out, row_grad, gate_total, up_total, down_total = lax.map(
        expert_pass, (rows, grads, gate_weight, up_weight, down_weight))
    flat = order.reshape(-1)
    combined = jnp.zeros((TOKENS, D), jnp.float32).at[flat].add(
        (gains[:, :, None] * expert_out.astype(jnp.float32)).reshape(-1, D))
    returned = jnp.zeros((TOKENS, D), jnp.float32).at[flat].add(
        row_grad.astype(jnp.float32).reshape(-1, D))
    return (combined.astype(jnp.bfloat16), returned.astype(jnp.bfloat16), gate_total, up_total, down_total)
```

```python
import functools

import jax
import jax.numpy as jnp
from jax import lax
from jax.experimental import pallas as pl
from jax.experimental.pallas import tpu as pltpu
from jax.sharding import PartitionSpec as P

CAP = 4
LANES = 128
F32 = jnp.float32
BF16 = jnp.bfloat16


def mm(left, right, left_dim=1, right_dim=0):
    return lax.dot_general(
        left, right, (((left_dim,), (right_dim,)), ((), ())), preferred_element_type=F32
    )


def iota(shape, dim):
    return lax.broadcasted_iota(jnp.int32, shape, dim)


def slots_of(ids, gates, experts):
    count = ids.shape[1]
    hit = ids < experts
    expert = jnp.sum(jnp.where(hit, ids, 0), axis=0, keepdims=True)
    held = jnp.max(jnp.where(hit, 1, 0), axis=0, keepdims=True) > 0
    gate = jnp.sum(jnp.where(hit, gates, 0.0), axis=0, keepdims=True)
    chosen = (iota((experts, count), 0) == expert) & held
    before = (iota((count, count), 0) < iota((count, count), 1)).astype(F32).astype(BF16)
    ranks = mm(chosen.astype(F32).astype(BF16), before)
    rank = jnp.sum(jnp.where(chosen, ranks, 0.0), axis=0, keepdims=True).astype(jnp.int32)
    slot = jnp.where(held, expert * (2 * CAP) + rank, -2 * CAP)
    rows = iota((experts * 2 * CAP, count), 0)
    row_hot = rows == slot
    grad_hot = rows == slot + CAP
    row_gate = jnp.sum(jnp.where(row_hot, gate, 0.0), axis=1, keepdims=True)
    grad_gate = jnp.sum(jnp.where(grad_hot, gate, 0.0), axis=1, keepdims=True)
    return row_hot.astype(F32).astype(BF16), grad_hot.astype(F32).astype(BF16), row_gate, grad_gate


def fill_rows(row_hot, grad_hot, grad_gate, tokens, cotangent):
    return (mm(row_hot, tokens) + grad_gate * mm(grad_hot, cotangent)).astype(BF16)


def combine(row_hot, grad_hot, row_gate, got):
    wide = got.astype(F32)
    is_row = iota(row_gate.shape, 0) % (2 * CAP) < CAP
    weighted = jnp.where(is_row, row_gate * wide, wide).astype(BF16)
    return mm(row_hot, weighted, 0, 0).astype(BF16), mm(grad_hot, weighted, 0, 0).astype(BF16)


def pickers(count):
    row = iota((count, 2 * count), 0)
    at = row // CAP * (2 * CAP) + row % CAP
    column = iota((count, 2 * count), 1)
    return (column == at).astype(F32).astype(BF16), (column == at + CAP).astype(F32).astype(BF16)


def nonlinear(partials, hidden):
    total = functools.reduce(lambda a, b: a + b, [part.astype(F32) for part in partials])
    pre_gate = total[:, :hidden]
    pre_up = total[:, hidden : 2 * hidden]
    hidden_grad = total[:, 2 * hidden :]
    squash = jax.nn.sigmoid(pre_gate)
    silu_gate = pre_gate * squash
    gate_grad = hidden_grad * pre_up * squash * (1.0 + pre_gate * (1.0 - squash))
    return jnp.concatenate(
        [
            gate_grad.astype(BF16),
            (hidden_grad * silu_gate).astype(BF16),
            (silu_gate * pre_up).astype(BF16),
        ],
        axis=1,
    )


def prep_kernel(experts, ids, gates, tokens, cotangent, out):
    row_hot, grad_hot, _, grad_gate = slots_of(ids[...], gates[...], experts)
    out[...] = fill_rows(row_hot, grad_hot, grad_gate, tokens[...], cotangent[...])


def prep(ids, gates, tokens, cotangent, experts, parts):
    count, width = tokens.shape
    piece = width // parts
    rows = experts * 2 * CAP
    if piece % LANES:
        row_hot, grad_hot, _, grad_gate = slots_of(ids, gates, experts)
        full = fill_rows(row_hot, grad_hot, grad_gate, tokens, cotangent)
        return full.reshape(rows, parts, piece).transpose(1, 0, 2)
    return pl.pallas_call(
        functools.partial(prep_kernel, experts),
        out_shape=jax.ShapeDtypeStruct((parts, rows, piece), BF16),
        grid=(parts,),
        in_specs=[
            pl.BlockSpec(ids.shape, lambda p: (0, 0)),
            pl.BlockSpec(gates.shape, lambda p: (0, 0)),
            pl.BlockSpec((count, piece), lambda p: (0, p)),
            pl.BlockSpec((count, piece), lambda p: (0, p)),
        ],
        out_specs=pl.BlockSpec((None, rows, piece), lambda p: (p, 0, 0)),
        name="prep",
    )(ids, gates, tokens, cotangent)


def finish_kernel(experts, ids, gates, got, out, grad):
    row_hot, grad_hot, row_gate, _ = slots_of(ids[...], gates[...], experts)
    out[...], grad[...] = combine(row_hot, grad_hot, row_gate, got[...])


def finish(ids, gates, got, experts):
    parts, rows, piece = got.shape
    count = ids.shape[1]
    if piece % LANES:
        row_hot, grad_hot, row_gate, _ = slots_of(ids, gates, experts)
        return combine(row_hot, grad_hot, row_gate, got.transpose(1, 0, 2).reshape(rows, parts * piece))
    shape = jax.ShapeDtypeStruct((count, parts * piece), BF16)
    spec = pl.BlockSpec((count, piece), lambda p: (0, p))
    return pl.pallas_call(
        functools.partial(finish_kernel, experts),
        out_shape=(shape, shape),
        grid=(parts,),
        in_specs=[
            pl.BlockSpec(ids.shape, lambda p: (0, 0)),
            pl.BlockSpec(gates.shape, lambda p: (0, 0)),
            pl.BlockSpec((None, rows, piece), lambda p: (p, 0, 0)),
        ],
        out_specs=(spec, spec),
        name="finish",
    )(ids, gates, got)


def forward_kernel(got, gate, up, down, pre_gate, pre_up, hidden_grad, rows, grads):
    @pl.when(pl.program_id(0) == 0)
    def _():
        pick_row, pick_grad = pickers(rows.shape[0])
        block = got[...]
        rows[...] = mm(pick_row, block).astype(BF16)
        grads[...] = mm(pick_grad, block).astype(BF16)

    pre_gate[...] = mm(rows[...], gate[...]).astype(BF16)
    pre_up[...] = mm(rows[...], up[...]).astype(BF16)
    hidden_grad[...] = mm(grads[...], down[...]).astype(BF16)


def forward(got, gate, up, down):
    total, piece = got.shape
    count = total // 2
    hidden = gate.shape[1]
    if piece % LANES:
        pick_row, pick_grad = pickers(count)
        rows = mm(pick_row, got).astype(BF16)
        grads = mm(pick_grad, got).astype(BF16)
        pre = jnp.concatenate([mm(rows, gate), mm(rows, up), mm(grads, down)], axis=1)
        return pre.astype(BF16), rows, grads
    step = 256
    weight = pl.BlockSpec((piece, step), lambda n: (0, n))
    kept = pl.BlockSpec((count, piece), lambda n: (0, 0))
    shape = jax.ShapeDtypeStruct((count, hidden), BF16)
    part = pl.BlockSpec((count, step), lambda n: (0, n))
    pre_gate, pre_up, hidden_grad, rows, grads = pl.pallas_call(
        forward_kernel,
        out_shape=(shape, shape, shape)
        + (jax.ShapeDtypeStruct((count, piece), BF16),) * 2,
        grid=(hidden // step,),
        in_specs=[pl.BlockSpec((total, piece), lambda n: (0, 0)), weight, weight, weight],
        out_specs=(part, part, part, kept, kept),
        name="forward",
    )(got, gate, up, down)
    return jnp.concatenate([pre_gate, pre_up, hidden_grad], axis=1), rows, grads


def middle_kernel(hidden, partials, out):
    out[...] = nonlinear([partials[k] for k in range(partials.shape[0])], hidden)


def middle(partials, hidden):
    _, rows, width = partials.shape
    return pl.pallas_call(
        functools.partial(middle_kernel, hidden),
        out_shape=jax.ShapeDtypeStruct((rows, width), BF16),
        name="middle",
    )(partials)


def backward_rows(acts, gate, up, down):
    hidden = gate.shape[1]
    out = mm(acts[:, 2 * hidden :], down, 1, 1).astype(BF16)
    back = (mm(acts[:, :hidden], gate, 1, 1) + mm(acts[:, hidden : 2 * hidden], up, 1, 1)).astype(BF16)
    pick_row, pick_grad = pickers(acts.shape[0])
    return (mm(pick_row, out, 0, 0) + mm(pick_grad, back, 0, 0)).astype(BF16)


def backward_kernel(acts, gate, up, down, out):
    out[...] = backward_rows(acts[...], gate[...], up[...], down[...])


def backward(acts, gate, up, down):
    count, width = acts.shape
    piece, hidden = gate.shape
    if piece % LANES:
        return backward_rows(acts, gate, up, down)
    step = 256
    weight = pl.BlockSpec((step, hidden), lambda d: (d, 0))
    return pl.pallas_call(
        backward_kernel,
        out_shape=jax.ShapeDtypeStruct((2 * count, piece), BF16),
        grid=(piece // step,),
        in_specs=[pl.BlockSpec((count, width), lambda d: (0, 0)), weight, weight, weight],
        out_specs=pl.BlockSpec((2 * count, step), lambda d: (0, d)),
        name="backward",
    )(acts, gate, up, down)


def weights_kernel(rows, grads, acts, gate, up, down):
    hidden = gate.shape[1]
    gate[...] = mm(rows[...], acts[:, :hidden], 0, 0).astype(BF16)
    up[...] = mm(rows[...], acts[:, hidden : 2 * hidden], 0, 0).astype(BF16)
    down[...] = mm(grads[...], acts[:, 2 * hidden :], 0, 0).astype(BF16)


def weights(rows, grads, acts, hidden):
    count, piece = rows.shape
    if piece % LANES:
        return (
            mm(rows, acts[:, :hidden], 0, 0).astype(BF16),
            mm(rows, acts[:, hidden : 2 * hidden], 0, 0).astype(BF16),
            mm(grads, acts[:, 2 * hidden :], 0, 0).astype(BF16),
        )
    step = 256
    shape = jax.ShapeDtypeStruct((piece, hidden), BF16)
    spec = pl.BlockSpec((step, hidden), lambda d: (d, 0))
    kept = pl.BlockSpec((count, step), lambda d: (0, d))
    return pl.pallas_call(
        weights_kernel,
        out_shape=(shape, shape, shape),
        grid=(piece // step,),
        in_specs=[kept, kept, pl.BlockSpec(acts.shape, lambda d: (0, 0))],
        out_specs=(spec, spec, spec),
        name="weights",
    )(rows, grads, acts)


def body(tokens, route_ids, gate_weights, gate_weight, up_weight, down_weight, cotangent):
    experts = lax.axis_size("expert")
    parts = lax.axis_size("dp")
    both = ("dp", "expert")
    gate, up, down = gate_weight[0], up_weight[0], down_weight[0]
    piece, hidden = gate.shape
    ids, gates = route_ids.T, gate_weights.T
    block = 2 * CAP

    sent = prep(ids, gates, tokens, cotangent, experts, parts)
    sent = sent.reshape(parts * experts, block, piece)
    got = lax.all_to_all(sent, both, 0, 0, tiled=True)
    pre, rows, grads = forward(got.reshape(parts * experts * block, piece), gate, up, down)
    mine = lax.all_to_all(pre.reshape(parts, experts * CAP, 3 * hidden), "dp", 0, 0, tiled=True)
    acts = lax.all_gather(middle(mine, hidden), "dp", axis=0, tiled=True)
    back = backward(acts, gate, up, down)
    back = lax.all_to_all(back.reshape(parts * experts, block, piece), both, 0, 0, tiled=True)
    totals = weights(rows, grads, acts, hidden)
    output, grad_tokens = finish(ids, gates, back.reshape(parts, experts * block, piece), experts)
    return (output, grad_tokens) + tuple(total[None] for total in totals)


def solution(mesh):
    rows = P(("dp", "expert"), None)
    held = P("expert", "dp", None)
    return jax.shard_map(
        body,
        mesh=mesh,
        in_specs=(rows, rows, rows, held, held, held, rows),
        out_specs=(rows, rows, held, held, held),
        check_vma=False,
    )
```

```python
import functools

import jax
import jax.numpy as jnp
from jax import lax
from jax.experimental import pallas as pl
from jax.experimental.pallas import tpu as pltpu
from jax.sharding import PartitionSpec as P

CAP = 4
LANES = 128
F32 = jnp.float32
BF16 = jnp.bfloat16


def mm(left, right, left_dim=1, right_dim=0):
    return lax.dot_general(
        left, right, (((left_dim,), (right_dim,)), ((), ())), preferred_element_type=F32
    )


def iota(shape, dim):
    return lax.broadcasted_iota(jnp.int32, shape, dim)


def slots_of(ids, gates, experts):
    count = ids.shape[1]
    hit = ids < experts
    expert = jnp.sum(jnp.where(hit, ids, 0), axis=0, keepdims=True)
    held = jnp.max(jnp.where(hit, 1, 0), axis=0, keepdims=True) > 0
    gate = jnp.sum(jnp.where(hit, gates, 0.0), axis=0, keepdims=True)
    chosen = (iota((experts, count), 0) == expert) & held
    before = (iota((count, count), 0) < iota((count, count), 1)).astype(F32).astype(BF16)
    ranks = mm(chosen.astype(F32).astype(BF16), before)
    rank = jnp.sum(jnp.where(chosen, ranks, 0.0), axis=0, keepdims=True).astype(jnp.int32)
    slot = jnp.where(held, expert * (2 * CAP) + rank, -2 * CAP)
    rows = iota((experts * 2 * CAP, count), 0)
    row_hot = rows == slot
    grad_hot = rows == slot + CAP
    row_gate = jnp.sum(jnp.where(row_hot, gate, 0.0), axis=1, keepdims=True)
    grad_gate = jnp.sum(jnp.where(grad_hot, gate, 0.0), axis=1, keepdims=True)
    return row_hot.astype(F32).astype(BF16), grad_hot.astype(F32).astype(BF16), row_gate, grad_gate


def fill_rows(row_hot, grad_hot, grad_gate, tokens, cotangent):
    return (mm(row_hot, tokens) + grad_gate * mm(grad_hot, cotangent)).astype(BF16)


def combine(row_hot, grad_hot, row_gate, got):
    wide = got.astype(F32)
    is_row = iota(row_gate.shape, 0) % (2 * CAP) < CAP
    weighted = jnp.where(is_row, row_gate * wide, wide).astype(BF16)
    return mm(row_hot, weighted, 0, 0).astype(BF16), mm(grad_hot, weighted, 0, 0).astype(BF16)


def pickers(count):
    row = iota((count, 2 * count), 0)
    at = row // CAP * (2 * CAP) + row % CAP
    column = iota((count, 2 * count), 1)
    return (column == at).astype(F32).astype(BF16), (column == at + CAP).astype(F32).astype(BF16)


def nonlinear(partials, hidden):
    total = functools.reduce(lambda a, b: a + b, [part.astype(F32) for part in partials])
    pre_gate = total[:, :hidden]
    pre_up = total[:, hidden : 2 * hidden]
    hidden_grad = total[:, 2 * hidden :]
    squash = jax.nn.sigmoid(pre_gate)
    silu_gate = pre_gate * squash
    gate_grad = hidden_grad * pre_up * squash * (1.0 + pre_gate * (1.0 - squash))
    return jnp.concatenate(
        [
            gate_grad.astype(BF16),
            (hidden_grad * silu_gate).astype(BF16),
            (silu_gate * pre_up).astype(BF16),
        ],
        axis=1,
    )


ROOM = pltpu.CompilerParams(vmem_limit_bytes=16 * 2**20)
IN_VMEM = pl.BlockSpec(memory_space=pltpu.VMEM)
IN_HBM = pl.BlockSpec(memory_space=pltpu.HBM)
DMA = pltpu.SemaphoreType.DMA


def in_hbm(x):
    return pltpu.with_memory_space_constraint(x, pltpu.HBM)


def like(shape):
    return jax.ShapeDtypeStruct(shape, BF16)


def prep_kernel(experts, ids, gates, tokens, cotangent, out, row_hot, grad_hot, row_gate, held, sems):
    parts, _, piece = out.shape
    copies = [
        [
            pltpu.make_async_copy(
                full.at[:, pl.ds(p * piece, piece)], held.at[k, p], sems.at[k, p]
            )
            for k, full in enumerate((tokens, cotangent))
        ]
        for p in range(parts)
    ]
    for pair in copies:
        for copy in pair:
            copy.start()
    row_hot[...], grad_hot[...], row_gate[...], grad_gate = slots_of(ids[...], gates[...], experts)
    for p, pair in enumerate(copies):
        for copy in pair:
            copy.wait()
        out[p] = fill_rows(row_hot[...], grad_hot[...], grad_gate, held[0, p], held[1, p])


def prep(ids, gates, tokens, cotangent, experts, parts):
    count, width = tokens.shape
    piece = width // parts
    rows = experts * 2 * CAP
    if piece % LANES:
        row_hot, grad_hot, row_gate, grad_gate = slots_of(ids, gates, experts)
        full = fill_rows(row_hot, grad_hot, grad_gate, tokens, cotangent)
        return full.reshape(rows, parts, piece).transpose(1, 0, 2), row_hot, grad_hot, row_gate
    hot = like((rows, count))
    return pl.pallas_call(
        functools.partial(prep_kernel, experts),
        out_shape=(like((parts, rows, piece)), hot, hot, jax.ShapeDtypeStruct((rows, 1), F32)),
        in_specs=[IN_VMEM, IN_VMEM, IN_HBM, IN_HBM],
        out_specs=(IN_VMEM,) * 4,
        scratch_shapes=[pltpu.VMEM((2, parts, count, piece), BF16), DMA((2, parts))],
        compiler_params=ROOM,
        name="prep",
    )(in_hbm(ids), in_hbm(gates), in_hbm(tokens), in_hbm(cotangent))


def finish_kernel(row_hot, grad_hot, row_gate, got, out, grad):
    block = got[pl.program_id(0)]
    out[...], grad[...] = combine(row_hot[...], grad_hot[...], row_gate[...], block)


def finish(row_hot, grad_hot, row_gate, got):
    parts, rows, piece = got.shape
    count = row_hot.shape[1]
    if piece % LANES:
        return combine(row_hot, grad_hot, row_gate, got.transpose(1, 0, 2).reshape(rows, parts * piece))
    shape = like((count, parts * piece))
    spec = pl.BlockSpec((count, piece), lambda p: (0, p))
    return pl.pallas_call(
        finish_kernel,
        out_shape=(shape, shape),
        grid=(parts,),
        in_specs=[IN_VMEM] * 4,
        out_specs=(spec, spec),
        compiler_params=ROOM,
        name="finish",
    )(row_hot, grad_hot, row_gate, got)


def split_rows(block):
    pick_row, pick_grad = pickers(block.shape[0] // 2)
    return mm(pick_row, block).astype(BF16), mm(pick_grad, block).astype(BF16)


def forward_kernel(got, gate, up, down, pre, rows, grads, held_up, held_down, sems):
    hidden = gate.shape[1]
    fetch_up = pltpu.make_async_copy(up, held_up, sems.at[0])
    fetch_down = pltpu.make_async_copy(down, held_down, sems.at[1])
    fetch_up.start()
    fetch_down.start()
    row_part, grad_part = split_rows(got[...])
    rows[...], grads[...] = row_part, grad_part
    pre[:, :hidden] = mm(row_part, gate[...]).astype(BF16)
    fetch_up.wait()
    pre[:, hidden : 2 * hidden] = mm(row_part, held_up[...]).astype(BF16)
    fetch_down.wait()
    pre[:, 2 * hidden :] = mm(grad_part, held_down[...]).astype(BF16)


def forward(got, gate, up, down):
    total, piece = got.shape
    count = total // 2
    hidden = gate.shape[1]
    if piece % LANES:
        rows, grads = split_rows(got)
        pre = jnp.concatenate([mm(rows, gate), mm(rows, up), mm(grads, down)], axis=1)
        return pre.astype(BF16), rows, grads, up, down
    kept = like((count, piece))
    return pl.pallas_call(
        forward_kernel,
        out_shape=(like((count, 3 * hidden)), kept, kept, like(up.shape), like(down.shape)),
        in_specs=[IN_VMEM, IN_VMEM, IN_HBM, IN_HBM],
        out_specs=(IN_VMEM,) * 5,
        scratch_shapes=[DMA((2,))],
        compiler_params=ROOM,
        name="forward",
    )(got, gate, in_hbm(up), in_hbm(down))


def middle_kernel(hidden, partials, out):
    out[...] = nonlinear([partials[k] for k in range(partials.shape[0])], hidden)


def middle(partials, hidden):
    _, rows, width = partials.shape
    return pl.pallas_call(
        functools.partial(middle_kernel, hidden),
        out_shape=like((rows, width)),
        in_specs=[IN_VMEM],
        out_specs=IN_VMEM,
        compiler_params=ROOM,
        name="middle",
    )(partials)


def backward_rows(acts, gate, up, down):
    hidden = gate.shape[1]
    pick_row, pick_grad = pickers(acts.shape[0])
    gate_grad = mm(pick_grad, acts[:, :hidden], 0, 0).astype(BF16)
    up_grad = mm(pick_grad, acts[:, hidden : 2 * hidden], 0, 0).astype(BF16)
    active = mm(pick_row, acts[:, 2 * hidden :], 0, 0).astype(BF16)
    total = mm(down, active, 1, 1) + mm(gate, gate_grad, 1, 1) + mm(up, up_grad, 1, 1)
    return total.astype(BF16).T


def backward_kernel(acts, gate, up, down, out):
    out[...] = backward_rows(acts[...], gate[...], up[...], down[...])


def backward(acts, gate, up, down):
    piece = gate.shape[0]
    if piece % LANES:
        return backward_rows(acts, gate, up, down)
    return pl.pallas_call(
        backward_kernel,
        out_shape=like((2 * acts.shape[0], piece)),
        in_specs=[IN_VMEM] * 4,
        out_specs=IN_VMEM,
        compiler_params=ROOM,
        name="backward",
    )(acts, gate, up, down)


def weights_kernel(rows, grads, acts, gate, up, down):
    hidden = gate.shape[1]
    gate[...] = mm(rows[...], acts[:, :hidden], 0, 0).astype(BF16)
    up[...] = mm(rows[...], acts[:, hidden : 2 * hidden], 0, 0).astype(BF16)
    down[...] = mm(grads[...], acts[:, 2 * hidden :], 0, 0).astype(BF16)


def weights(rows, grads, acts, hidden):
    count, piece = rows.shape
    if piece % LANES:
        return (
            mm(rows, acts[:, :hidden], 0, 0).astype(BF16),
            mm(rows, acts[:, hidden : 2 * hidden], 0, 0).astype(BF16),
            mm(grads, acts[:, 2 * hidden :], 0, 0).astype(BF16),
        )
    step = 2 * LANES
    shape = like((piece, hidden))
    spec = pl.BlockSpec((step, hidden), lambda d: (d, 0))
    kept = pl.BlockSpec((count, step), lambda d: (0, d))
    return pl.pallas_call(
        weights_kernel,
        out_shape=(shape, shape, shape),
        grid=(piece // step,),
        in_specs=[kept, kept, pl.BlockSpec(acts.shape, lambda d: (0, 0))],
        out_specs=(spec, spec, spec),
        compiler_params=ROOM,
        name="weights",
    )(rows, grads, acts)


def body(tokens, route_ids, gate_weights, gate_weight, up_weight, down_weight, cotangent):
    experts = lax.axis_size("expert")
    parts = lax.axis_size("dp")
    both = ("dp", "expert")
    gate, up, down = gate_weight[0], up_weight[0], down_weight[0]
    piece, hidden = gate.shape
    ids, gates = route_ids.T, gate_weights.T
    block = 2 * CAP

    sent, row_hot, grad_hot, row_gate = prep(ids, gates, tokens, cotangent, experts, parts)
    sent = sent.reshape(parts * experts, block, piece)
    got = lax.all_to_all(sent, both, 0, 0, tiled=True)
    got = got.reshape(parts * experts * block, piece)
    pre, rows, grads, up, down = forward(got, gate, up, down)
    mine = lax.all_to_all(pre.reshape(parts, experts * CAP, 3 * hidden), "dp", 0, 0, tiled=True)
    acts = lax.all_gather(middle(mine, hidden), "dp", axis=0, tiled=True)
    back = backward(acts, gate, up, down)
    back = lax.all_to_all(back.reshape(parts * experts, block, piece), both, 0, 0, tiled=True)
    totals = weights(rows, grads, acts, hidden)
    back = back.reshape(parts, experts * block, piece)
    output, grad_tokens = finish(row_hot, grad_hot, row_gate, back)
    return (output, grad_tokens) + tuple(total[None] for total in totals)


def solution(mesh):
    rows = P(("dp", "expert"), None)
    held = P("expert", "dp", None)
    return jax.shard_map(
        body,
        mesh=mesh,
        in_specs=(rows, rows, rows, held, held, held, rows),
        out_specs=(rows, rows, held, held, held),
        check_vma=False,
    )
```

```python
import functools

import jax
import jax.numpy as jnp
from jax import lax
from jax.experimental import pallas as pl
from jax.experimental.pallas import tpu as pltpu
from jax.sharding import PartitionSpec as P


CAP = 4
LANES = 128
F32 = jnp.float32
BF16 = jnp.bfloat16


def mm(left, right, left_dim=1, right_dim=0):
    return lax.dot_general(
        left, right, (((left_dim,), (right_dim,)), ((), ())), preferred_element_type=F32
    )


def iota(shape, dim):
    return lax.broadcasted_iota(jnp.int32, shape, dim)


def slots_of(ids, gates, experts):
    count = ids.shape[1]
    hit = ids < experts
    expert = jnp.sum(jnp.where(hit, ids, 0), axis=0, keepdims=True)
    held = jnp.max(jnp.where(hit, 1, 0), axis=0, keepdims=True) > 0
    gate = jnp.sum(jnp.where(hit, gates, 0.0), axis=0, keepdims=True)
    chosen = (iota((experts, count), 0) == expert) & held
    before = (iota((count, count), 0) < iota((count, count), 1)).astype(F32).astype(BF16)
    ranks = mm(chosen.astype(F32).astype(BF16), before)
    rank = jnp.sum(jnp.where(chosen, ranks, 0.0), axis=0, keepdims=True).astype(jnp.int32)
    slot = jnp.where(held, expert * (2 * CAP) + rank, -2 * CAP)
    rows = iota((experts * 2 * CAP, count), 0)
    row_hot = rows == slot
    grad_hot = rows == slot + CAP
    row_gate = jnp.sum(jnp.where(row_hot, gate, 0.0), axis=1, keepdims=True)
    grad_gate = jnp.sum(jnp.where(grad_hot, gate, 0.0), axis=1, keepdims=True)
    return row_hot.astype(F32).astype(BF16), grad_hot.astype(F32).astype(BF16), row_gate, grad_gate


def fill_rows(row_hot, grad_hot, grad_gate, tokens, cotangent):
    return (mm(row_hot, tokens) + grad_gate * mm(grad_hot, cotangent)).astype(BF16)


def combine(row_hot, grad_hot, row_gate, got):
    wide = got.astype(F32)
    is_row = iota(row_gate.shape, 0) % (2 * CAP) < CAP
    weighted = jnp.where(is_row, row_gate * wide, wide).astype(BF16)
    return mm(row_hot, weighted, 0, 0).astype(BF16), mm(grad_hot, weighted, 0, 0).astype(BF16)


def pickers(count, me=0, group=None):
    row = iota((count, 2 * count), 0)
    if group is not None:
        row = ((row // group) ^ me) * group + row % group
    at = row // CAP * (2 * CAP) + row % CAP
    column = iota((count, 2 * count), 1)
    return (column == at).astype(F32).astype(BF16), (column == at + CAP).astype(F32).astype(BF16)


def add_up(parts):
    return functools.reduce(lambda a, b: a + b, [part.astype(F32) for part in parts])


def hidden_of(pre, hidden):
    pre_gate = pre[:, :hidden]
    return (pre_gate * jax.nn.sigmoid(pre_gate) * pre[:, hidden:]).astype(BF16)


def grads_of(pre, hidden_grad, hidden):
    pre_gate = pre[:, :hidden]
    pre_up = pre[:, hidden:]
    squash = jax.nn.sigmoid(pre_gate)
    gate_grad = hidden_grad * pre_up * squash * (1.0 + pre_gate * (1.0 - squash))
    up_grad = hidden_grad * (pre_gate * squash)
    return jnp.concatenate([gate_grad.astype(BF16), up_grad.astype(BF16)], axis=1)


def plain_middle(me, got, gate, up, down):
    count = got.shape[0] // 2
    hidden = gate.shape[1]
    pick_row, pick_grad = pickers(count)
    rows = mm(pick_row, got).astype(BF16)
    grads = mm(pick_grad, got).astype(BF16)
    pre = jnp.concatenate([mm(rows, gate), mm(rows, up), mm(grads, down)], axis=1).astype(BF16)
    parts = lax.axis_size("dp")
    mine = lax.all_to_all(pre.reshape(parts, count // parts, 3 * hidden), "dp", 0, 0, tiled=True)
    total = add_up([mine[k] for k in range(parts)])
    pair = total[:, : 2 * hidden]
    acts = jnp.concatenate(
        [grads_of(pair, total[:, 2 * hidden :], hidden), hidden_of(pair, hidden)], axis=1
    )
    acts = lax.all_gather(acts, "dp", axis=0, tiled=True)
    gate_grad, up_grad, active = (acts[:, i * hidden : (i + 1) * hidden] for i in range(3))
    out = mm(active, down, 1, 1).astype(BF16)
    back = (mm(gate_grad, gate, 1, 1) + mm(up_grad, up, 1, 1)).astype(BF16)
    sent = (mm(pick_row, out, 0, 0) + mm(pick_grad, back, 0, 0)).astype(BF16)
    totals = (
        mm(rows, gate_grad, 0, 0).astype(BF16),
        mm(rows, up_grad, 0, 0).astype(BF16),
        mm(grads, active, 0, 0).astype(BF16),
    )
    return sent, totals


ROOM = pltpu.CompilerParams(vmem_limit_bytes=16 * 2**20)
IN_VMEM = pl.BlockSpec(memory_space=pltpu.VMEM)
IN_HBM = pl.BlockSpec(memory_space=pltpu.HBM)
IN_SMEM = pl.BlockSpec(memory_space=pltpu.SMEM)
DMA = pltpu.SemaphoreType.DMA


def in_hbm(x):
    return pltpu.with_memory_space_constraint(x, pltpu.HBM)


def like(shape):
    return jax.ShapeDtypeStruct(shape, BF16)


def prep_kernel(experts, me, ids, gates, tokens, cotangent, out, row_hot, grad_hot, row_gate, held, sems):
    del me
    parts, _, piece = out.shape
    copies = [
        [
            pltpu.make_async_copy(
                full.at[:, pl.ds(p * piece, piece)], held.at[k, p], sems.at[k, p]
            )
            for k, full in enumerate((tokens, cotangent))
        ]
        for p in range(parts)
    ]
    for pair in copies:
        for copy in pair:
            copy.start()
    row_hot[...], grad_hot[...], row_gate[...], grad_gate = slots_of(ids[...], gates[...], experts)
    for p, pair in enumerate(copies):
        for copy in pair:
            copy.wait()
        out[p] = fill_rows(row_hot[...], grad_hot[...], grad_gate, held[0, p], held[1, p])


def prep(me, ids, gates, tokens, cotangent, experts, parts):
    count, width = tokens.shape
    piece = width // parts
    rows = experts * 2 * CAP
    if piece % LANES:
        row_hot, grad_hot, row_gate, grad_gate = slots_of(ids, gates, experts)
        full = fill_rows(row_hot, grad_hot, grad_gate, tokens, cotangent)
        return full.reshape(rows, parts, piece).transpose(1, 0, 2), row_hot, grad_hot, row_gate
    hot = like((rows, count))
    return pl.pallas_call(
        functools.partial(prep_kernel, experts),
        out_shape=(like((parts, rows, piece)), hot, hot, jax.ShapeDtypeStruct((rows, 1), F32)),
        in_specs=[IN_SMEM, IN_VMEM, IN_VMEM, IN_HBM, IN_HBM],
        out_specs=(IN_VMEM,) * 4,
        scratch_shapes=[pltpu.VMEM((2, parts, count, piece), BF16), DMA((2, parts))],
        compiler_params=ROOM,
        name="prep",
    )(me, in_hbm(ids), in_hbm(gates), in_hbm(tokens), in_hbm(cotangent))


def finish_kernel(row_hot, grad_hot, row_gate, got, out, grad):
    block = got[pl.program_id(0)]
    out[...], grad[...] = combine(row_hot[...], grad_hot[...], row_gate[...], block)


def finish(row_hot, grad_hot, row_gate, got):
    parts, rows, piece = got.shape
    count = row_hot.shape[1]
    if piece % LANES:
        return combine(row_hot, grad_hot, row_gate, got.transpose(1, 0, 2).reshape(rows, parts * piece))
    shape = like((count, parts * piece))
    spec = pl.BlockSpec((count, piece), lambda p: (0, p))
    return pl.pallas_call(
        finish_kernel,
        out_shape=(shape, shape),
        grid=(parts,),
        in_specs=[IN_VMEM] * 4,
        out_specs=(spec, spec),
        compiler_params=ROOM,
        name="finish",
    )(row_hot, grad_hot, row_gate, got)


def blocks_of(value, refs):
    group = refs[0].shape[0]
    for k, ref in enumerate(refs):
        ref[...] = value[k * group : (k + 1) * group]


def rows_kernel(parts, me, got, gate, up, rows, *rest):
    sent, (held_up, sem) = rest[:parts], rest[parts:]
    fetch = pltpu.make_async_copy(up, held_up, sem)
    fetch.start()
    count = rows.shape[0]
    pick, _ = pickers(count, me[0], count // parts)
    part = mm(pick, got[...]).astype(BF16)
    rows[...] = part
    first = mm(part, gate[...]).astype(BF16)
    fetch.wait()
    blocks_of(jnp.concatenate([first, mm(part, held_up[...]).astype(BF16)], axis=1), sent)


def grads_kernel(parts, me, got, down, rows, *rest):
    sent, (held_down, sem) = rest[:parts], rest[parts:]
    fetch = pltpu.make_async_copy(down, held_down, sem)
    fetch.start()
    count = rows.shape[0]
    _, pick = pickers(count, me[0], count // parts)
    part = mm(pick, got[...]).astype(BF16)
    rows[...] = part
    fetch.wait()
    blocks_of(mm(part, held_down[...]).astype(BF16), sent)


def hidden_kernel(hidden, count, *refs):
    refs[-1][...] = hidden_of(add_up([part[...] for part in refs[:count]]), hidden)


def grad_kernel(hidden, count, *refs):
    pre = add_up([part[...] for part in refs[:count]])
    hidden_grad = add_up([part[...] for part in refs[count : 2 * count]])
    refs[-1][...] = grads_of(pre, hidden_grad, hidden)


def stacked(refs):
    return jnp.concatenate([ref[...] for ref in refs], axis=0)


def output_kernel(parts, me, *refs):
    active = stacked(refs[:parts])
    down, out = refs[parts:]
    pick, _ = pickers(active.shape[0], me[0], active.shape[0] // parts)
    spread = mm(pick, active, 0, 0).astype(BF16)
    out[...] = mm(down[...], spread, 1, 1).astype(BF16).T


def back_kernel(parts, me, *refs):
    acts = stacked(refs[:parts])
    gate, up, first, out = refs[parts:]
    hidden = gate.shape[1]
    _, pick = pickers(acts.shape[0], me[0], acts.shape[0] // parts)
    spread = mm(pick, acts, 0, 0).astype(BF16)
    total = mm(gate[...], spread[:, :hidden], 1, 1) + mm(up[...], spread[:, hidden:], 1, 1)
    out[...] = total.astype(BF16).T + first[...]


def weights_kernel(parts, rows, grads, *refs):
    actives, acts = refs[:parts], refs[parts : 2 * parts]
    gate, up, down, held_active, held = refs[2 * parts :]
    hidden = gate.shape[1]

    @pl.when(pl.program_id(0) == 0)
    def _():
        held_active[...] = stacked(actives)
        held[...] = stacked(acts)

    gate[...] = mm(rows[...], held[:, :hidden], 0, 0).astype(BF16)
    up[...] = mm(rows[...], held[:, hidden:], 0, 0).astype(BF16)
    down[...] = mm(grads[...], held_active[...], 0, 0).astype(BF16)


def run(kernel, outs, args, hbm=(), scratch=()):
    specs = [
        IN_SMEM
        if x.shape == (1,)
        else IN_HBM
        if i in hbm
        else IN_VMEM
        for i, x in enumerate(args)
    ]
    return pl.pallas_call(
        kernel,
        out_shape=tuple(like(shape) for shape in outs),
        in_specs=specs,
        out_specs=(IN_VMEM,) * len(outs),
        scratch_shapes=list(scratch),
        compiler_params=ROOM,
    )(*(in_hbm(x) if i in hbm else x for i, x in enumerate(args)))


def to_all(blocks):
    parts = len(blocks)
    moved = {
        k: lax.ppermute(blocks[k], "dp", [(i, i ^ k) for i in range(parts)])
        for k in range(parts - 1, 0, -1)
    }
    return [blocks[0]] + [moved[k] for k in range(1, parts)]


def tiled_middle(me, got, gate, up, down):
    total, piece = got.shape
    count = total // 2
    hidden = gate.shape[1]
    parts = lax.axis_size("dp")
    group = count // parts
    part = functools.partial

    held = [pltpu.VMEM((piece, hidden), BF16), DMA]
    rows, *sent = run(
        part(rows_kernel, parts),
        ((count, piece),) + ((group, 2 * hidden),) * parts,
        (me, got, gate, up),
        hbm=(3,),
        scratch=held,
    )
    pre = to_all(sent)
    grads, *sent = run(
        part(grads_kernel, parts),
        ((count, piece),) + ((group, hidden),) * parts,
        (me, got, down),
        hbm=(2,),
        scratch=held,
    )
    hidden_grad = to_all(sent)
    (active,) = run(part(hidden_kernel, hidden, parts), ((group, hidden),), (*pre, sent[0]))
    actives = to_all([active] * parts)
    (acts,) = run(part(grad_kernel, hidden, parts), ((group, 2 * hidden),), (*pre, *hidden_grad, active))
    acts = to_all([acts] * parts)
    (first,) = run(part(output_kernel, parts), ((total, piece),), (me, *actives, down))
    (back,) = run(part(back_kernel, parts), ((total, piece),), (me, *acts, gate, up, first))

    step = 2 * LANES
    spec = pl.BlockSpec((step, hidden), lambda d: (d, 0))
    kept = pl.BlockSpec((count, step), lambda d: (0, d))
    totals = pl.pallas_call(
        part(weights_kernel, parts),
        out_shape=(like((piece, hidden)),) * 3,
        grid=(piece // step,),
        in_specs=[kept, kept] + [IN_VMEM] * (2 * parts),
        out_specs=(spec, spec, spec),
        scratch_shapes=[pltpu.VMEM((count, hidden), BF16), pltpu.VMEM((count, 2 * hidden), BF16)],
        compiler_params=ROOM,
        name="weights",
    )(rows, grads, *actives, *acts)
    return back, totals


def body(tokens, route_ids, gate_weights, gate_weight, up_weight, down_weight, cotangent):
    experts = lax.axis_size("expert")
    parts = lax.axis_size("dp")
    both = ("dp", "expert")
    gate, up, down = gate_weight[0], up_weight[0], down_weight[0]
    piece = gate.shape[0]
    ids, gates = route_ids.T, gate_weights.T
    block = 2 * CAP

    me = lax.axis_index("dp").astype(jnp.int32).reshape(1)
    sent, row_hot, grad_hot, row_gate = prep(me, ids, gates, tokens, cotangent, experts, parts)
    sent = sent.reshape(parts * experts, block, piece)
    got = lax.all_to_all(sent, both, 0, 0, tiled=True)
    got = got.reshape(parts * experts * block, piece)
    tiled = piece % (2 * LANES) == 0 and parts & (parts - 1) == 0
    back, totals = (tiled_middle if tiled else plain_middle)(me, got, gate, up, down)
    back = lax.all_to_all(back.reshape(parts * experts, block, piece), both, 0, 0, tiled=True)
    back = back.reshape(parts, experts * block, piece)
    output, grad_tokens = finish(row_hot, grad_hot, row_gate, back)
    return (output, grad_tokens) + tuple(total[None] for total in totals)


def solution(mesh):
    rows = P(("dp", "expert"), None)
    held = P("expert", "dp", None)
    return jax.shard_map(
        body,
        mesh=mesh,
        in_specs=(rows, rows, rows, held, held, held, rows),
        out_specs=(rows, rows, held, held, held),
        check_vma=False,
    )
```

```python
import functools

import jax
import jax.numpy as jnp
from jax import lax
from jax.experimental import pallas as pl
from jax.experimental.pallas import tpu as pltpu
from jax.sharding import PartitionSpec as P


CAP = 4
LANES = 128
F32 = jnp.float32
BF16 = jnp.bfloat16


def mm(left, right, left_dim=1, right_dim=0):
    return lax.dot_general(
        left, right, (((left_dim,), (right_dim,)), ((), ())), preferred_element_type=F32
    )


def iota(shape, dim):
    return lax.broadcasted_iota(jnp.int32, shape, dim)


def slots_of(ids, gates, experts):
    count = ids.shape[1]
    hit = ids < experts
    expert = jnp.sum(jnp.where(hit, ids, 0), axis=0, keepdims=True)
    held = jnp.max(jnp.where(hit, 1, 0), axis=0, keepdims=True) > 0
    gate = jnp.sum(jnp.where(hit, gates, 0.0), axis=0, keepdims=True)
    chosen = (iota((experts, count), 0) == expert) & held
    before = (iota((count, count), 0) < iota((count, count), 1)).astype(F32).astype(BF16)
    ranks = mm(chosen.astype(F32).astype(BF16), before)
    rank = jnp.sum(jnp.where(chosen, ranks, 0.0), axis=0, keepdims=True).astype(jnp.int32)
    slot = jnp.where(held, expert * (2 * CAP) + rank, -2 * CAP)
    rows = iota((experts * 2 * CAP, count), 0)
    row_hot = rows == slot
    grad_hot = rows == slot + CAP
    row_gate = jnp.sum(jnp.where(row_hot, gate, 0.0), axis=1, keepdims=True)
    grad_gate = jnp.sum(jnp.where(grad_hot, gate, 0.0), axis=1, keepdims=True)
    return row_hot.astype(F32).astype(BF16), grad_hot.astype(F32).astype(BF16), row_gate, grad_gate


def fill_rows(row_hot, grad_hot, grad_gate, tokens, cotangent):
    return (mm(row_hot, tokens) + grad_gate * mm(grad_hot, cotangent)).astype(BF16)


def combine(row_hot, grad_hot, row_gate, got):
    wide = got.astype(F32)
    is_row = iota(row_gate.shape, 0) % (2 * CAP) < CAP
    weighted = jnp.where(is_row, row_gate * wide, wide).astype(BF16)
    return mm(row_hot, weighted, 0, 0).astype(BF16), mm(grad_hot, weighted, 0, 0).astype(BF16)


def pickers(count, me=0, group=None):
    row = iota((count, 2 * count), 0)
    if group is not None:
        row = ((row // group) ^ me) * group + row % group
    at = row // CAP * (2 * CAP) + row % CAP
    column = iota((count, 2 * count), 1)
    return (column == at).astype(F32).astype(BF16), (column == at + CAP).astype(F32).astype(BF16)


def add_up(parts):
    return functools.reduce(lambda a, b: a + b, [part.astype(F32) for part in parts])


def hidden_of(pre, hidden):
    pre_gate = pre[:, :hidden]
    return (pre_gate * jax.nn.sigmoid(pre_gate) * pre[:, hidden:]).astype(BF16)


def grads_of(pre, hidden_grad, hidden):
    pre_gate = pre[:, :hidden]
    pre_up = pre[:, hidden:]
    squash = jax.nn.sigmoid(pre_gate)
    gate_grad = hidden_grad * pre_up * squash * (1.0 + pre_gate * (1.0 - squash))
    up_grad = hidden_grad * (pre_gate * squash)
    return jnp.concatenate([gate_grad.astype(BF16), up_grad.astype(BF16)], axis=1)


def plain_middle(me, got, gate, up, down):
    count = got.shape[0] // 2
    hidden = gate.shape[1]
    pick_row, pick_grad = pickers(count)
    rows = mm(pick_row, got).astype(BF16)
    grads = mm(pick_grad, got).astype(BF16)
    pre = jnp.concatenate([mm(rows, gate), mm(rows, up), mm(grads, down)], axis=1).astype(BF16)
    parts = lax.axis_size("dp")
    mine = lax.all_to_all(pre.reshape(parts, count // parts, 3 * hidden), "dp", 0, 0, tiled=True)
    total = add_up([mine[k] for k in range(parts)])
    pair = total[:, : 2 * hidden]
    acts = jnp.concatenate(
        [grads_of(pair, total[:, 2 * hidden :], hidden), hidden_of(pair, hidden)], axis=1
    )
    acts = lax.all_gather(acts, "dp", axis=0, tiled=True)
    gate_grad, up_grad, active = (acts[:, i * hidden : (i + 1) * hidden] for i in range(3))
    out = mm(active, down, 1, 1).astype(BF16)
    back = (mm(gate_grad, gate, 1, 1) + mm(up_grad, up, 1, 1)).astype(BF16)
    sent = (mm(pick_row, out, 0, 0) + mm(pick_grad, back, 0, 0)).astype(BF16)
    totals = (
        mm(rows, gate_grad, 0, 0).astype(BF16),
        mm(rows, up_grad, 0, 0).astype(BF16),
        mm(grads, active, 0, 0).astype(BF16),
    )
    return sent, totals


ROOM = pltpu.CompilerParams(vmem_limit_bytes=16 * 2**20)
IN_VMEM = pl.BlockSpec(memory_space=pltpu.VMEM)
IN_HBM = pl.BlockSpec(memory_space=pltpu.HBM)
IN_SMEM = pl.BlockSpec(memory_space=pltpu.SMEM)
DMA = pltpu.SemaphoreType.DMA


def in_hbm(x):
    return pltpu.with_memory_space_constraint(x, pltpu.HBM)


def like(shape):
    return jax.ShapeDtypeStruct(shape, BF16)


def prep_kernel(experts, me, ids, gates, tokens, cotangent, out, row_hot, grad_hot, row_gate, held, sems):
    del me
    parts, _, piece = out.shape
    copies = [
        [
            pltpu.make_async_copy(
                full.at[:, pl.ds(p * piece, piece)], held.at[k, p], sems.at[k, p]
            )
            for k, full in enumerate((tokens, cotangent))
        ]
        for p in range(parts)
    ]
    for pair in copies:
        for copy in pair:
            copy.start()
    row_hot[...], grad_hot[...], row_gate[...], grad_gate = slots_of(ids[...], gates[...], experts)
    for p, pair in enumerate(copies):
        for copy in pair:
            copy.wait()
        out[p] = fill_rows(row_hot[...], grad_hot[...], grad_gate, held[0, p], held[1, p])


def prep(me, ids, gates, tokens, cotangent, experts, parts):
    count, width = tokens.shape
    piece = width // parts
    rows = experts * 2 * CAP
    if piece % LANES:
        row_hot, grad_hot, row_gate, grad_gate = slots_of(ids, gates, experts)
        full = fill_rows(row_hot, grad_hot, grad_gate, tokens, cotangent)
        return full.reshape(rows, parts, piece).transpose(1, 0, 2), row_hot, grad_hot, row_gate
    hot = like((rows, count))
    return pl.pallas_call(
        functools.partial(prep_kernel, experts),
        out_shape=(like((parts, rows, piece)), hot, hot, jax.ShapeDtypeStruct((rows, 1), F32)),
        in_specs=[IN_SMEM, IN_VMEM, IN_VMEM, IN_HBM, IN_HBM],
        out_specs=(IN_VMEM,) * 4,
        scratch_shapes=[pltpu.VMEM((2, parts, count, piece), BF16), DMA((2, parts))],
        compiler_params=ROOM,
        name="prep",
    )(me, in_hbm(ids), in_hbm(gates), in_hbm(tokens), in_hbm(cotangent))


def finish_kernel(row_hot, grad_hot, row_gate, got, out, grad, held, sems):
    parts, _, piece = got.shape
    copies = []
    for p in range(parts):
        held[0, p], held[1, p] = combine(row_hot[...], grad_hot[...], row_gate[...], got[p])
        for k, full in enumerate((out, grad)):
            copy = pltpu.make_async_copy(
                held.at[k, p], full.at[:, pl.ds(p * piece, piece)], sems.at[k, p]
            )
            copy.start()
            copies.append(copy)
    for copy in copies:
        copy.wait()


def finish(row_hot, grad_hot, row_gate, got):
    parts, rows, piece = got.shape
    count = row_hot.shape[1]
    if piece % LANES:
        return combine(row_hot, grad_hot, row_gate, got.transpose(1, 0, 2).reshape(rows, parts * piece))
    shape = pltpu.HBM((count, parts * piece), BF16)
    return pl.pallas_call(
        finish_kernel,
        out_shape=(shape, shape),
        in_specs=[IN_VMEM] * 4,
        out_specs=(IN_HBM, IN_HBM),
        scratch_shapes=[pltpu.VMEM((2, parts, count, piece), BF16), DMA((2, parts))],
        compiler_params=ROOM,
        name="finish",
    )(row_hot, grad_hot, row_gate, got)


def blocks_of(value, refs):
    group = refs[0].shape[0]
    for k, ref in enumerate(refs):
        ref[...] = value[k * group : (k + 1) * group]


def rows_kernel(parts, me, got, gate, up, rows, *rest):
    sent, (held_up, sem) = rest[:parts], rest[parts:]
    fetch = pltpu.make_async_copy(up, held_up, sem)
    fetch.start()
    count = rows.shape[0]
    pick, _ = pickers(count, me[0], count // parts)
    part = mm(pick, got[...]).astype(BF16)
    rows[...] = part
    first = mm(part, gate[...]).astype(BF16)
    fetch.wait()
    blocks_of(jnp.concatenate([first, mm(part, held_up[...]).astype(BF16)], axis=1), sent)


def grads_kernel(parts, me, got, down, rows, *sent):
    count = rows.shape[0]
    _, pick = pickers(count, me[0], count // parts)
    part = mm(pick, got[...]).astype(BF16)
    rows[...] = part
    blocks_of(mm(part, down[...]).astype(BF16), sent)


def hidden_kernel(hidden, count, *refs):
    refs[-1][...] = hidden_of(add_up([part[...] for part in refs[:count]]), hidden)


def grad_kernel(hidden, count, *refs):
    pre = add_up([part[...] for part in refs[:count]])
    hidden_grad = add_up([part[...] for part in refs[count : 2 * count]])
    refs[-1][...] = grads_of(pre, hidden_grad, hidden)


def stacked(refs):
    return jnp.concatenate([ref[...] for ref in refs], axis=0)


def weave(count, me, group):
    row = iota((2 * count, 2 * count), 0)
    kind = row // CAP % 2
    place = row // (2 * CAP) * CAP + row % CAP
    source = kind * count + ((place // group) ^ me) * group + place % group
    return (iota((2 * count, 2 * count), 1) == source).astype(F32).astype(BF16)


def output_kernel(parts, me, *refs):
    active = stacked(refs[:parts])
    down, gate, up, out, gate_turned, up_turned, woven = refs[parts:]
    count = active.shape[0]
    out[...] = mm(active, down[...], 1, 1).astype(BF16)
    woven[...] = weave(count, me[0], count // parts)
    gate_turned[...] = gate[...].T
    up_turned[...] = up[...].T


def back_kernel(parts, *refs):
    acts = stacked(refs[:parts])
    gate_turned, up_turned, first, woven, out = refs[parts:]
    hidden = gate_turned.shape[0]
    total = mm(acts[:, :hidden], gate_turned[...]) + mm(acts[:, hidden:], up_turned[...])
    both = jnp.concatenate([first[...], total.astype(BF16)], axis=0)
    out[...] = mm(woven[...], both).astype(BF16)


def weights_kernel(parts, rows, grads, *refs):
    actives, acts = refs[:parts], refs[parts : 2 * parts]
    gate, up, down, held_active, held = refs[2 * parts :]
    hidden = gate.shape[1]

    @pl.when(pl.program_id(0) == 0)
    def _():
        held_active[...] = stacked(actives)
        held[...] = stacked(acts)

    gate[...] = mm(rows[...], held[:, :hidden], 0, 0).astype(BF16)
    up[...] = mm(rows[...], held[:, hidden:], 0, 0).astype(BF16)
    down[...] = mm(grads[...], held_active[...], 0, 0).astype(BF16)


def run(kernel, outs, args, hbm=(), scratch=()):
    specs = [
        IN_SMEM
        if x.shape == (1,)
        else IN_HBM
        if i in hbm
        else IN_VMEM
        for i, x in enumerate(args)
    ]
    return pl.pallas_call(
        kernel,
        out_shape=tuple(like(shape) for shape in outs),
        in_specs=specs,
        out_specs=(IN_VMEM,) * len(outs),
        scratch_shapes=list(scratch),
        compiler_params=ROOM,
    )(*(in_hbm(x) if i in hbm else x for i, x in enumerate(args)))


def to_all(blocks):
    parts = len(blocks)
    moved = {
        k: lax.ppermute(blocks[k], "dp", [(i, i ^ k) for i in range(parts)])
        for k in range(parts - 1, 0, -1)
    }
    return [blocks[0]] + [moved[k] for k in range(1, parts)]


def tiled_middle(me, got, gate, up, down):
    total, piece = got.shape
    count = total // 2
    hidden = gate.shape[1]
    parts = lax.axis_size("dp")
    group = count // parts
    part = functools.partial

    held = [pltpu.VMEM((piece, hidden), BF16), DMA]
    rows, *sent = run(
        part(rows_kernel, parts),
        ((count, piece),) + ((group, 2 * hidden),) * parts,
        (me, got, gate, up),
        hbm=(3,),
        scratch=held,
    )
    pre = to_all(sent)
    grads, *sent = run(part(grads_kernel, parts), ((count, piece),) + ((group, hidden),) * parts, (me, got, down))
    hidden_grad = to_all(sent)
    (active,) = run(part(hidden_kernel, hidden, parts), ((group, hidden),), (*pre, sent[0]))
    actives = to_all([active] * parts)
    (acts,) = run(part(grad_kernel, hidden, parts), ((group, 2 * hidden),), (*pre, *hidden_grad, active))
    acts = to_all([acts] * parts)
    turned = (hidden, piece)
    first, gate_turned, up_turned, woven = run(
        part(output_kernel, parts), ((count, piece), turned, turned, (total, total)), (me, *actives, down, gate, up)
    )
    (back,) = run(part(back_kernel, parts), ((total, piece),), (*acts, gate_turned, up_turned, first, woven))

    step = 2 * LANES
    spec = pl.BlockSpec((step, hidden), lambda d: (d, 0))
    kept = pl.BlockSpec((count, step), lambda d: (0, d))
    totals = pl.pallas_call(
        part(weights_kernel, parts),
        out_shape=(like((piece, hidden)),) * 3,
        grid=(piece // step,),
        in_specs=[kept, kept] + [IN_VMEM] * (2 * parts),
        out_specs=(spec, spec, spec),
        scratch_shapes=[pltpu.VMEM((count, hidden), BF16), pltpu.VMEM((count, 2 * hidden), BF16)],
        compiler_params=ROOM,
        name="weights",
    )(rows, grads, *actives, *acts)
    return back, totals


def body(tokens, route_ids, gate_weights, gate_weight, up_weight, down_weight, cotangent):
    experts = lax.axis_size("expert")
    parts = lax.axis_size("dp")
    both = ("dp", "expert")
    gate, up, down = gate_weight[0], up_weight[0], down_weight[0]
    piece = gate.shape[0]
    ids, gates = route_ids.T, gate_weights.T
    block = 2 * CAP

    me = lax.axis_index("dp").astype(jnp.int32).reshape(1)
    sent, row_hot, grad_hot, row_gate = prep(me, ids, gates, tokens, cotangent, experts, parts)
    sent = sent.reshape(parts * experts, block, piece)
    got = lax.all_to_all(sent, both, 0, 0, tiled=True)
    got = got.reshape(parts * experts * block, piece)
    tiled = piece % (2 * LANES) == 0 and parts & (parts - 1) == 0
    back, totals = (tiled_middle if tiled else plain_middle)(me, got, gate, up, down)
    back = lax.all_to_all(back.reshape(parts * experts, block, piece), both, 0, 0, tiled=True)
    back = back.reshape(parts, experts * block, piece)
    output, grad_tokens = finish(row_hot, grad_hot, row_gate, back)
    return (output, grad_tokens) + tuple(total[None] for total in totals)


def solution(mesh):
    rows = P(("dp", "expert"), None)
    held = P("expert", "dp", None)
    return jax.shard_map(
        body,
        mesh=mesh,
        in_specs=(rows, rows, rows, held, held, held, rows),
        out_specs=(rows, rows, held, held, held),
        check_vma=False,
    )
```

```python
import functools

import jax
import jax.numpy as jnp
from jax import lax
from jax.experimental import pallas as pl
from jax.experimental.pallas import tpu as pltpu
from jax.sharding import PartitionSpec as P


CAP = 4
LANES = 128
F32 = jnp.float32
BF16 = jnp.bfloat16


def mm(left, right, left_dim=1, right_dim=0):
    return lax.dot_general(
        left, right, (((left_dim,), (right_dim,)), ((), ())), preferred_element_type=F32
    )


def iota(shape, dim):
    return lax.broadcasted_iota(jnp.int32, shape, dim)


def slots_of(ids, gates, experts):
    count = ids.shape[1]
    hit = ids < experts
    expert = jnp.sum(jnp.where(hit, ids, 0), axis=0, keepdims=True)
    held = jnp.max(jnp.where(hit, 1, 0), axis=0, keepdims=True) > 0
    gate = jnp.sum(jnp.where(hit, gates, 0.0), axis=0, keepdims=True)
    chosen = (iota((experts, count), 0) == expert) & held
    before = (iota((count, count), 0) < iota((count, count), 1)).astype(F32).astype(BF16)
    ranks = mm(chosen.astype(F32).astype(BF16), before)
    rank = jnp.sum(jnp.where(chosen, ranks, 0.0), axis=0, keepdims=True).astype(jnp.int32)
    slot = jnp.where(held, expert * (2 * CAP) + rank, -2 * CAP)
    rows = iota((experts * 2 * CAP, count), 0)
    row_hot = rows == slot
    grad_hot = rows == slot + CAP
    row_gate = jnp.sum(jnp.where(row_hot, gate, 0.0), axis=1, keepdims=True)
    grad_gate = jnp.sum(jnp.where(grad_hot, gate, 0.0), axis=1, keepdims=True)
    return row_hot.astype(F32).astype(BF16), grad_hot.astype(F32).astype(BF16), row_gate, grad_gate


def fill_rows(row_hot, grad_hot, grad_gate, tokens, cotangent):
    return (mm(row_hot, tokens) + grad_gate * mm(grad_hot, cotangent)).astype(BF16)


def combine(row_hot, grad_hot, row_gate, got):
    wide = got.astype(F32)
    is_row = iota(row_gate.shape, 0) % (2 * CAP) < CAP
    weighted = jnp.where(is_row, row_gate * wide, wide).astype(BF16)
    return mm(row_hot, weighted, 0, 0).astype(BF16), mm(grad_hot, weighted, 0, 0).astype(BF16)


def pickers(count, me=0, group=None):
    row = iota((count, 2 * count), 0)
    if group is not None:
        row = ((row // group) ^ me) * group + row % group
    at = row // CAP * (2 * CAP) + row % CAP
    column = iota((count, 2 * count), 1)
    return (column == at).astype(F32).astype(BF16), (column == at + CAP).astype(F32).astype(BF16)


def add_up(parts):
    return functools.reduce(lambda a, b: a + b, [part.astype(F32) for part in parts])


def hidden_of(pre, hidden):
    pre_gate = pre[:, :hidden]
    return (pre_gate * jax.nn.sigmoid(pre_gate) * pre[:, hidden:]).astype(BF16)


def grads_of(pre, hidden_grad, hidden):
    pre_gate = pre[:, :hidden]
    pre_up = pre[:, hidden:]
    squash = jax.nn.sigmoid(pre_gate)
    gate_grad = hidden_grad * pre_up * squash * (1.0 + pre_gate * (1.0 - squash))
    up_grad = hidden_grad * (pre_gate * squash)
    return jnp.concatenate([gate_grad.astype(BF16), up_grad.astype(BF16)], axis=1)


def plain_middle(got, gate, up, down):
    count = got.shape[0] // 2
    hidden = gate.shape[1]
    pick_row, pick_grad = pickers(count)
    rows = mm(pick_row, got).astype(BF16)
    grads = mm(pick_grad, got).astype(BF16)
    pre = jnp.concatenate([mm(rows, gate), mm(rows, up), mm(grads, down)], axis=1).astype(BF16)
    parts = lax.axis_size("dp")
    mine = lax.all_to_all(pre.reshape(parts, count // parts, 3 * hidden), "dp", 0, 0, tiled=True)
    total = add_up([mine[k] for k in range(parts)])
    pair = total[:, : 2 * hidden]
    acts = jnp.concatenate(
        [grads_of(pair, total[:, 2 * hidden :], hidden), hidden_of(pair, hidden)], axis=1
    )
    acts = lax.all_gather(acts, "dp", axis=0, tiled=True)
    gate_grad, up_grad, active = (acts[:, i * hidden : (i + 1) * hidden] for i in range(3))
    out = mm(active, down, 1, 1).astype(BF16)
    back = (mm(gate_grad, gate, 1, 1) + mm(up_grad, up, 1, 1)).astype(BF16)
    sent = (mm(pick_row, out, 0, 0) + mm(pick_grad, back, 0, 0)).astype(BF16)
    totals = (
        mm(rows, gate_grad, 0, 0).astype(BF16),
        mm(rows, up_grad, 0, 0).astype(BF16),
        mm(grads, active, 0, 0).astype(BF16),
    )
    return sent, totals


ROOM = pltpu.CompilerParams(vmem_limit_bytes=16 * 2**20)
IN_VMEM = pl.BlockSpec(memory_space=pltpu.VMEM)
IN_HBM = pl.BlockSpec(memory_space=pltpu.HBM)
DMA = pltpu.SemaphoreType.DMA


def in_hbm(x):
    return pltpu.with_memory_space_constraint(x, pltpu.HBM)


def like(shape):
    return jax.ShapeDtypeStruct(shape, BF16)


def prep_kernel(
    experts,
    ids,
    gates,
    tokens,
    cotangent,
    out,
    row_hot,
    grad_hot,
    row_gate,
    held_ids,
    held_gates,
    held,
    small,
    sems,
):
    parts, _, piece = out.shape
    routes = [
        pltpu.make_async_copy(ids, held_ids, small.at[0]),
        pltpu.make_async_copy(gates, held_gates, small.at[1]),
    ]
    copies = [
        [
            pltpu.make_async_copy(
                full.at[:, pl.ds(p * piece, piece)], held.at[k, p], sems.at[k, p]
            )
            for k, full in enumerate((tokens, cotangent))
        ]
        for p in range(parts)
    ]
    for copy in routes + [copy for pair in copies for copy in pair]:
        copy.start()
    for copy in routes:
        copy.wait()
    row_hot[...], grad_hot[...], row_gate[...], grad_gate = slots_of(
        held_ids[...], held_gates[...], experts
    )
    for p, pair in enumerate(copies):
        for copy in pair:
            copy.wait()
        out[p] = fill_rows(row_hot[...], grad_hot[...], grad_gate, held[0, p], held[1, p])


def prep(ids, gates, tokens, cotangent, experts, parts):
    count, width = tokens.shape
    piece = width // parts
    rows = experts * 2 * CAP
    if piece % LANES:
        row_hot, grad_hot, row_gate, grad_gate = slots_of(ids, gates, experts)
        full = fill_rows(row_hot, grad_hot, grad_gate, tokens, cotangent)
        return full.reshape(rows, parts, piece).transpose(1, 0, 2), row_hot, grad_hot, row_gate
    hot = like((rows, count))
    return pl.pallas_call(
        functools.partial(prep_kernel, experts),
        out_shape=(like((parts, rows, piece)), hot, hot, jax.ShapeDtypeStruct((rows, 1), F32)),
        in_specs=[IN_HBM] * 4,
        out_specs=(IN_VMEM,) * 4,
        scratch_shapes=[
            pltpu.VMEM(ids.shape, ids.dtype),
            pltpu.VMEM(gates.shape, gates.dtype),
            pltpu.VMEM((2, parts, count, piece), BF16),
            DMA((2,)),
            DMA((2, parts)),
        ],
        compiler_params=ROOM,
        name="prep",
    )(in_hbm(ids), in_hbm(gates), in_hbm(tokens), in_hbm(cotangent))


def finish_kernel(row_hot, grad_hot, row_gate, got, out, grad, held, sems):
    parts, _, piece = got.shape
    copies = []
    for p in range(parts):
        held[0, p], held[1, p] = combine(row_hot[...], grad_hot[...], row_gate[...], got[p])
        for k, full in enumerate((out, grad)):
            copy = pltpu.make_async_copy(
                held.at[k, p], full.at[:, pl.ds(p * piece, piece)], sems.at[k, p]
            )
            copy.start()
            copies.append(copy)
    for copy in copies:
        copy.wait()


def finish(row_hot, grad_hot, row_gate, got):
    parts, rows, piece = got.shape
    count = row_hot.shape[1]
    if piece % LANES:
        return combine(row_hot, grad_hot, row_gate, got.transpose(1, 0, 2).reshape(rows, parts * piece))
    shape = pltpu.HBM((count, parts * piece), BF16)
    return pl.pallas_call(
        finish_kernel,
        out_shape=(shape, shape),
        in_specs=[IN_VMEM] * 4,
        out_specs=(IN_HBM, IN_HBM),
        scratch_shapes=[pltpu.VMEM((2, parts, count, piece), BF16), DMA((2, parts))],
        compiler_params=ROOM,
        name="finish",
    )(row_hot, grad_hot, row_gate, got)


def blocks_of(value, refs):
    group = refs[0].shape[0]
    for k, ref in enumerate(refs):
        ref[...] = value[k * group : (k + 1) * group]


def rows_kernel(parts, got, gate, up, rows, held_up, *rest):
    sent, sem = rest[:parts], rest[parts]
    fetch = pltpu.make_async_copy(up, held_up, sem)
    fetch.start()
    count, hidden = rows.shape[0], gate.shape[1]
    pick, _ = pickers(count, lax.axis_index("dp"), count // parts)
    part = mm(pick, got[...]).astype(BF16)
    rows[...] = part
    blocks_of(mm(part, gate[...]).astype(BF16), [ref.at[:, :hidden] for ref in sent])
    fetch.wait()
    blocks_of(mm(part, held_up[...]).astype(BF16), [ref.at[:, hidden:] for ref in sent])


def grads_kernel(parts, got, down, after, rows, held_down, *rest):
    sent, sem = rest[:parts], rest[parts]
    fetch = pltpu.make_async_copy(down, held_down, sem)
    fetch.start()
    count = rows.shape[0]
    _, pick = pickers(count, lax.axis_index("dp"), count // parts)
    part = mm(pick, got[...]).astype(BF16)
    rows[...] = part
    fetch.wait()
    blocks_of(mm(part, held_down[...]).astype(BF16), sent)


def hidden_kernel(hidden, count, *refs):
    refs[-1][...] = hidden_of(add_up([part[...] for part in refs[:count]]), hidden)


def grad_kernel(hidden, count, *refs):
    pre = add_up([part[...] for part in refs[:count]])
    hidden_grad = add_up([part[...] for part in refs[count : 2 * count]])
    refs[-1][...] = grads_of(pre, hidden_grad, hidden)


def stacked(refs):
    return jnp.concatenate([ref[...] for ref in refs], axis=0)


def weave(count, me, group):
    row = iota((2 * count, 2 * count), 0)
    kind = row // CAP % 2
    place = row // (2 * CAP) * CAP + row % CAP
    source = kind * count + ((place // group) ^ me) * group + place % group
    return (iota((2 * count, 2 * count), 1) == source).astype(F32).astype(BF16)


def output_kernel(parts, *refs):
    active = stacked(refs[:parts])
    down, gate, up, out, gate_turned, up_turned, woven = refs[parts:]
    count = active.shape[0]
    out[...] = mm(active, down[...], 1, 1).astype(BF16)
    woven[...] = weave(count, lax.axis_index("dp"), count // parts)
    gate_turned[...] = gate[...].T
    up_turned[...] = up[...].T


def back_kernel(parts, *refs):
    acts = stacked(refs[:parts])
    gate_turned, up_turned, first, woven, out = refs[parts:]
    hidden = gate_turned.shape[0]
    total = mm(acts[:, :hidden], gate_turned[...]) + mm(acts[:, hidden:], up_turned[...])
    both = jnp.concatenate([first[...], total.astype(BF16)], axis=0)
    out[...] = mm(woven[...], both).astype(BF16)


def weights_kernel(parts, rows, grads, *refs):
    actives, acts = refs[:parts], refs[parts : 2 * parts]
    gate, up, down, held_active, held = refs[2 * parts :]
    hidden = gate.shape[1]

    @pl.when(pl.program_id(0) == 0)
    def _():
        held_active[...] = stacked(actives)
        held[...] = stacked(acts)

    gate[...] = mm(rows[...], held[:, :hidden], 0, 0).astype(BF16)
    up[...] = mm(rows[...], held[:, hidden:], 0, 0).astype(BF16)
    down[...] = mm(grads[...], held_active[...], 0, 0).astype(BF16)


def run(kernel, outs, args, hbm=(), scratch=()):
    specs = [IN_HBM if i in hbm else IN_VMEM for i in range(len(args))]
    return pl.pallas_call(
        kernel,
        out_shape=tuple(like(shape) for shape in outs),
        in_specs=specs,
        out_specs=(IN_VMEM,) * len(outs),
        scratch_shapes=list(scratch),
        compiler_params=ROOM,
    )(*(in_hbm(x) if i in hbm else x for i, x in enumerate(args)))


def to_all(blocks):
    parts = len(blocks)
    moved = {
        k: lax.ppermute(blocks[k], "dp", [(i, i ^ k) for i in range(parts)])
        for k in range(parts - 1, 0, -1)
    }
    return [blocks[0]] + [moved[k] for k in range(1, parts)]


def tiled_middle(got, gate, up, down):
    total, piece = got.shape
    count = total // 2
    hidden = gate.shape[1]
    parts = lax.axis_size("dp")
    group = count // parts
    part = functools.partial

    rows, up, *sent = run(
        part(rows_kernel, parts),
        ((count, piece), up.shape) + ((group, 2 * hidden),) * parts,
        (got, gate, up),
        hbm=(2,),
        scratch=(DMA,),
    )
    pre = to_all(sent)
    grads, down, *sent = run(
        part(grads_kernel, parts),
        ((count, piece), down.shape) + ((group, hidden),) * parts,
        (got, down, sent[0]),
        hbm=(1,),
        scratch=(DMA,),
    )
    hidden_grad = to_all(sent)
    (active,) = run(part(hidden_kernel, hidden, parts), ((group, hidden),), (*pre, sent[0]))
    actives = to_all([active] * parts)
    (acts,) = run(
        part(grad_kernel, hidden, parts), ((group, 2 * hidden),), (*pre, *hidden_grad, active)
    )
    acts = to_all([acts] * parts)
    turned = (hidden, piece)
    first, gate_turned, up_turned, woven = run(
        part(output_kernel, parts),
        ((count, piece), turned, turned, (total, total)),
        (*actives, down, gate, up),
    )
    (back,) = run(
        part(back_kernel, parts), ((total, piece),), (*acts, gate_turned, up_turned, first, woven)
    )

    step = 2 * LANES
    spec = pl.BlockSpec((step, hidden), lambda d: (d, 0))
    kept = pl.BlockSpec((count, step), lambda d: (0, d))
    totals = pl.pallas_call(
        part(weights_kernel, parts),
        out_shape=(like((piece, hidden)),) * 3,
        grid=(piece // step,),
        in_specs=[kept, kept] + [IN_VMEM] * (2 * parts),
        out_specs=(spec, spec, spec),
        scratch_shapes=[pltpu.VMEM((count, hidden), BF16), pltpu.VMEM((count, 2 * hidden), BF16)],
        compiler_params=ROOM,
        name="weights",
    )(rows, grads, *actives, *acts)
    return back, totals


def body(tokens, route_ids, gate_weights, gate_weight, up_weight, down_weight, cotangent):
    experts = lax.axis_size("expert")
    parts = lax.axis_size("dp")
    both = ("dp", "expert")
    gate, up, down = gate_weight[0], up_weight[0], down_weight[0]
    piece = gate.shape[0]
    ids, gates = route_ids.T, gate_weights.T
    block = 2 * CAP

    sent, row_hot, grad_hot, row_gate = prep(ids, gates, tokens, cotangent, experts, parts)
    sent = sent.reshape(parts * experts, block, piece)
    got = lax.all_to_all(sent, both, 0, 0, tiled=True)
    got = got.reshape(parts * experts * block, piece)
    tiled = piece % (2 * LANES) == 0 and parts & (parts - 1) == 0
    back, totals = (tiled_middle if tiled else plain_middle)(got, gate, up, down)
    back = lax.all_to_all(back.reshape(parts * experts, block, piece), both, 0, 0, tiled=True)
    back = back.reshape(parts, experts * block, piece)
    output, grad_tokens = finish(row_hot, grad_hot, row_gate, back)
    return (output, grad_tokens) + tuple(total[None] for total in totals)


def solution(mesh):
    rows = P(("dp", "expert"), None)
    held = P("expert", "dp", None)
    return jax.shard_map(
        body,
        mesh=mesh,
        in_specs=(rows, rows, rows, held, held, held, rows),
        out_specs=(rows, rows, held, held, held),
        check_vma=False,
    )
```

```python
import functools

import jax
import jax.numpy as jnp
from jax import lax
from jax.experimental import pallas as pl
from jax.experimental.pallas import tpu as pltpu
from jax.sharding import PartitionSpec as P


CAP = 4
LANES = 128
F32 = jnp.float32
BF16 = jnp.bfloat16


def mm(left, right, left_dim=1, right_dim=0):
    return lax.dot_general(
        left, right, (((left_dim,), (right_dim,)), ((), ())), preferred_element_type=F32
    )


def iota(shape, dim):
    return lax.broadcasted_iota(jnp.int32, shape, dim)


def slots_of(ids, gates, experts):
    count = ids.shape[1]
    hit = ids < experts
    expert = jnp.sum(jnp.where(hit, ids, 0), axis=0, keepdims=True)
    held = jnp.max(jnp.where(hit, 1, 0), axis=0, keepdims=True) > 0
    gate = jnp.sum(jnp.where(hit, gates, 0.0), axis=0, keepdims=True)
    chosen = (iota((experts, count), 0) == expert) & held
    before = (iota((count, count), 0) < iota((count, count), 1)).astype(F32).astype(BF16)
    ranks = mm(chosen.astype(F32).astype(BF16), before)
    rank = jnp.sum(jnp.where(chosen, ranks, 0.0), axis=0, keepdims=True).astype(jnp.int32)
    slot = jnp.where(held, expert * (2 * CAP) + rank, -2 * CAP)
    rows = iota((experts * 2 * CAP, count), 0)
    row_hot = rows == slot
    grad_hot = rows == slot + CAP
    row_gate = jnp.sum(jnp.where(row_hot, gate, 0.0), axis=1, keepdims=True)
    grad_gate = jnp.sum(jnp.where(grad_hot, gate, 0.0), axis=1, keepdims=True)
    return row_hot.astype(F32).astype(BF16), grad_hot.astype(F32).astype(BF16), row_gate, grad_gate


def fill_rows(row_hot, grad_hot, grad_gate, tokens, cotangent):
    return (mm(row_hot, tokens) + grad_gate * mm(grad_hot, cotangent)).astype(BF16)


def combine(row_hot, grad_hot, row_gate, got):
    wide = got.astype(F32)
    is_row = iota(row_gate.shape, 0) % (2 * CAP) < CAP
    weighted = jnp.where(is_row, row_gate * wide, wide).astype(BF16)
    return mm(row_hot, weighted, 0, 0).astype(BF16), mm(grad_hot, weighted, 0, 0).astype(BF16)


def pickers(count, me=0, group=None):
    row = iota((count, 2 * count), 0)
    if group is not None:
        row = ((row // group) ^ me) * group + row % group
    at = row // CAP * (2 * CAP) + row % CAP
    column = iota((count, 2 * count), 1)
    return (column == at).astype(F32).astype(BF16), (column == at + CAP).astype(F32).astype(BF16)


def add_up(parts):
    return functools.reduce(lambda a, b: a + b, [part.astype(F32) for part in parts])


def hidden_of(pre, hidden):
    pre_gate = pre[:, :hidden]
    return (pre_gate * jax.nn.sigmoid(pre_gate) * pre[:, hidden:]).astype(BF16)


def grads_of(pre, hidden_grad, hidden):
    pre_gate = pre[:, :hidden]
    pre_up = pre[:, hidden:]
    squash = jax.nn.sigmoid(pre_gate)
    gate_grad = hidden_grad * pre_up * squash * (1.0 + pre_gate * (1.0 - squash))
    up_grad = hidden_grad * (pre_gate * squash)
    return jnp.concatenate([gate_grad.astype(BF16), up_grad.astype(BF16)], axis=1)


def plain_middle(got, gate, up, down):
    count = got.shape[0] // 2
    hidden = gate.shape[1]
    pick_row, pick_grad = pickers(count)
    rows = mm(pick_row, got).astype(BF16)
    grads = mm(pick_grad, got).astype(BF16)
    pre = jnp.concatenate([mm(rows, gate), mm(rows, up), mm(grads, down)], axis=1).astype(BF16)
    parts = lax.axis_size("dp")
    mine = lax.all_to_all(pre.reshape(parts, count // parts, 3 * hidden), "dp", 0, 0, tiled=True)
    total = add_up([mine[k] for k in range(parts)])
    pair = total[:, : 2 * hidden]
    acts = jnp.concatenate(
        [grads_of(pair, total[:, 2 * hidden :], hidden), hidden_of(pair, hidden)], axis=1
    )
    acts = lax.all_gather(acts, "dp", axis=0, tiled=True)
    gate_grad, up_grad, active = (acts[:, i * hidden : (i + 1) * hidden] for i in range(3))
    out = mm(active, down, 1, 1).astype(BF16)
    back = (mm(gate_grad, gate, 1, 1) + mm(up_grad, up, 1, 1)).astype(BF16)
    sent = (mm(pick_row, out, 0, 0) + mm(pick_grad, back, 0, 0)).astype(BF16)
    totals = (
        mm(rows, gate_grad, 0, 0).astype(BF16),
        mm(rows, up_grad, 0, 0).astype(BF16),
        mm(grads, active, 0, 0).astype(BF16),
    )
    return sent, totals


ROOM = pltpu.CompilerParams(vmem_limit_bytes=16 * 2**20)
IN_VMEM = pl.BlockSpec(memory_space=pltpu.VMEM)
IN_HBM = pl.BlockSpec(memory_space=pltpu.HBM)
DMA = pltpu.SemaphoreType.DMA


def in_hbm(x):
    return pltpu.with_memory_space_constraint(x, pltpu.HBM)


def like(shape):
    return jax.ShapeDtypeStruct(shape, BF16)


def prep_kernel(
    experts,
    ids,
    gates,
    tokens,
    cotangent,
    out,
    row_hot,
    grad_hot,
    row_gate,
    held_ids,
    held_gates,
    held,
    small,
    sems,
):
    parts, _, piece = out.shape
    routes = [
        pltpu.make_async_copy(ids, held_ids, small.at[0]),
        pltpu.make_async_copy(gates, held_gates, small.at[1]),
    ]
    copies = [
        [
            pltpu.make_async_copy(
                full.at[:, pl.ds(p * piece, piece)], held.at[k, p], sems.at[k, p]
            )
            for k, full in enumerate((tokens, cotangent))
        ]
        for p in range(parts)
    ]
    for copy in routes + [copy for pair in copies for copy in pair]:
        copy.start()
    for copy in routes:
        copy.wait()
    row_hot[...], grad_hot[...], row_gate[...], grad_gate = slots_of(
        held_ids[...], held_gates[...], experts
    )
    for p, pair in enumerate(copies):
        for copy in pair:
            copy.wait()
        out[p] = fill_rows(row_hot[...], grad_hot[...], grad_gate, held[0, p], held[1, p])


def prep(ids, gates, tokens, cotangent, experts, parts):
    count, width = tokens.shape
    piece = width // parts
    rows = experts * 2 * CAP
    if piece % LANES:
        row_hot, grad_hot, row_gate, grad_gate = slots_of(ids, gates, experts)
        full = fill_rows(row_hot, grad_hot, grad_gate, tokens, cotangent)
        return full.reshape(rows, parts, piece).transpose(1, 0, 2), row_hot, grad_hot, row_gate
    hot = like((rows, count))
    return pl.pallas_call(
        functools.partial(prep_kernel, experts),
        out_shape=(like((parts, rows, piece)), hot, hot, jax.ShapeDtypeStruct((rows, 1), F32)),
        in_specs=[IN_HBM] * 4,
        out_specs=(IN_VMEM,) * 4,
        scratch_shapes=[
            pltpu.VMEM(ids.shape, ids.dtype),
            pltpu.VMEM(gates.shape, gates.dtype),
            pltpu.VMEM((2, parts, count, piece), BF16),
            DMA((2,)),
            DMA((2, parts)),
        ],
        compiler_params=ROOM,
        name="prep",
    )(in_hbm(ids), in_hbm(gates), in_hbm(tokens), in_hbm(cotangent))


def finish_kernel(row_hot, grad_hot, row_gate, got, out, grad, held, sems):
    parts, _, piece = got.shape
    copies = []
    for p in range(parts):
        held[0, p], held[1, p] = combine(row_hot[...], grad_hot[...], row_gate[...], got[p])
        for k, full in enumerate((out, grad)):
            copy = pltpu.make_async_copy(
                held.at[k, p], full.at[:, pl.ds(p * piece, piece)], sems.at[k, p]
            )
            copy.start()
            copies.append(copy)
    for copy in copies:
        copy.wait()


def finish(row_hot, grad_hot, row_gate, got):
    parts, rows, piece = got.shape
    count = row_hot.shape[1]
    if piece % LANES:
        return combine(row_hot, grad_hot, row_gate, got.transpose(1, 0, 2).reshape(rows, parts * piece))
    shape = pltpu.HBM((count, parts * piece), BF16)
    return pl.pallas_call(
        finish_kernel,
        out_shape=(shape, shape),
        in_specs=[IN_VMEM] * 4,
        out_specs=(IN_HBM, IN_HBM),
        scratch_shapes=[pltpu.VMEM((2, parts, count, piece), BF16), DMA((2, parts))],
        compiler_params=ROOM,
        name="finish",
    )(row_hot, grad_hot, row_gate, got)


def blocks_of(value, refs):
    group = refs[0].shape[0]
    for k, ref in enumerate(refs):
        ref[...] = value[k * group : (k + 1) * group]


def rows_kernel(parts, got, gate, up, rows, held_up, *rest):
    sent, sem = rest[:parts], rest[parts]
    fetch = pltpu.make_async_copy(up, held_up, sem)
    fetch.start()
    count, hidden = rows.shape[0], gate.shape[1]
    pick, _ = pickers(count, lax.axis_index("dp"), count // parts)
    part = mm(pick, got[...]).astype(BF16)
    rows[...] = part
    blocks_of(mm(part, gate[...]).astype(BF16), [ref.at[:, :hidden] for ref in sent])
    fetch.wait()
    blocks_of(mm(part, held_up[...]).astype(BF16), [ref.at[:, hidden:] for ref in sent])


def grads_kernel(parts, got, down, after, rows, held_down, *rest):
    sent, sem = rest[:parts], rest[parts]
    fetch = pltpu.make_async_copy(down, held_down, sem)
    fetch.start()
    count = rows.shape[0]
    _, pick = pickers(count, lax.axis_index("dp"), count // parts)
    part = mm(pick, got[...]).astype(BF16)
    rows[...] = part
    fetch.wait()
    blocks_of(mm(part, held_down[...]).astype(BF16), sent)


def hidden_kernel(hidden, count, *refs):
    refs[-1][...] = hidden_of(add_up([part[...] for part in refs[:count]]), hidden)


def grad_kernel(hidden, count, *refs):
    pre = add_up([part[...] for part in refs[:count]])
    hidden_grad = add_up([part[...] for part in refs[count : 2 * count]])
    refs[-1][...] = grads_of(pre, hidden_grad, hidden)


def stacked(refs):
    return jnp.concatenate([ref[...] for ref in refs], axis=0)


def weave(count, me, group):
    row = iota((2 * count, 2 * count), 0)
    kind = row // CAP % 2
    place = row // (2 * CAP) * CAP + row % CAP
    source = kind * count + ((place // group) ^ me) * group + place % group
    return (iota((2 * count, 2 * count), 1) == source).astype(F32).astype(BF16)


def output_kernel(parts, *refs):
    active = stacked(refs[:parts])
    down, gate, up, out, turned, woven = refs[parts:]
    hidden = gate.shape[1]
    count = active.shape[0]
    out[...] = mm(active, down[...], 1, 1).astype(BF16)
    woven[...] = weave(count, lax.axis_index("dp"), count // parts)
    turned[:hidden] = gate[...].T
    turned[hidden:] = up[...].T


def back_kernel(parts, *refs):
    acts = stacked(refs[:parts])
    turned, first, woven, out = refs[parts:]
    total = mm(acts, turned[...])
    both = jnp.concatenate([first[...], total.astype(BF16)], axis=0)
    out[...] = mm(woven[...], both).astype(BF16)


def weights_kernel(parts, rows, grads, *refs):
    actives, acts = refs[:parts], refs[parts : 2 * parts]
    gate, up, down, held_active, held = refs[2 * parts :]
    hidden = gate.shape[1]

    @pl.when(pl.program_id(0) == 0)
    def _():
        held_active[...] = stacked(actives)
        held[...] = stacked(acts)

    gate[...] = mm(rows[...], held[:, :hidden], 0, 0).astype(BF16)
    up[...] = mm(rows[...], held[:, hidden:], 0, 0).astype(BF16)
    down[...] = mm(grads[...], held_active[...], 0, 0).astype(BF16)


def run(kernel, outs, args, hbm=(), scratch=()):
    specs = [IN_HBM if i in hbm else IN_VMEM for i in range(len(args))]
    return pl.pallas_call(
        kernel,
        out_shape=tuple(like(shape) for shape in outs),
        in_specs=specs,
        out_specs=(IN_VMEM,) * len(outs),
        scratch_shapes=list(scratch),
        compiler_params=ROOM,
    )(*(in_hbm(x) if i in hbm else x for i, x in enumerate(args)))


def to_all(blocks):
    parts = len(blocks)
    moved = {
        k: lax.ppermute(blocks[k], "dp", [(i, i ^ k) for i in range(parts)])
        for k in range(parts - 1, 0, -1)
    }
    return [blocks[0]] + [moved[k] for k in range(1, parts)]


def tiled_middle(got, gate, up, down):
    total, piece = got.shape
    count = total // 2
    hidden = gate.shape[1]
    parts = lax.axis_size("dp")
    group = count // parts
    part = functools.partial

    rows, up, *sent = run(
        part(rows_kernel, parts),
        ((count, piece), up.shape) + ((group, 2 * hidden),) * parts,
        (got, gate, up),
        hbm=(2,),
        scratch=(DMA,),
    )
    pre = to_all(sent)
    grads, down, *sent = run(
        part(grads_kernel, parts),
        ((count, piece), down.shape) + ((group, hidden),) * parts,
        (got, down, sent[0]),
        hbm=(1,),
        scratch=(DMA,),
    )
    hidden_grad = to_all(sent)
    (active,) = run(part(hidden_kernel, hidden, parts), ((group, hidden),), (*pre, sent[0]))
    actives = to_all([active] * parts)
    (acts,) = run(
        part(grad_kernel, hidden, parts), ((group, 2 * hidden),), (*pre, *hidden_grad, active)
    )
    acts = to_all([acts] * parts)
    first, turned, woven = run(
        part(output_kernel, parts),
        ((count, piece), (2 * hidden, piece), (total, total)),
        (*actives, down, gate, up),
    )
    (back,) = run(part(back_kernel, parts), ((total, piece),), (*acts, turned, first, woven))

    step = 2 * LANES
    spec = pl.BlockSpec((step, hidden), lambda d: (d, 0))
    kept = pl.BlockSpec((count, step), lambda d: (0, d))
    totals = pl.pallas_call(
        part(weights_kernel, parts),
        out_shape=(like((piece, hidden)),) * 3,
        grid=(piece // step,),
        in_specs=[kept, kept] + [IN_VMEM] * (2 * parts),
        out_specs=(spec, spec, spec),
        scratch_shapes=[pltpu.VMEM((count, hidden), BF16), pltpu.VMEM((count, 2 * hidden), BF16)],
        compiler_params=ROOM,
        name="weights",
    )(rows, grads, *actives, *acts)
    return back, totals


def body(tokens, route_ids, gate_weights, gate_weight, up_weight, down_weight, cotangent):
    experts = lax.axis_size("expert")
    parts = lax.axis_size("dp")
    both = ("dp", "expert")
    gate, up, down = gate_weight[0], up_weight[0], down_weight[0]
    piece = gate.shape[0]
    ids, gates = route_ids.T, gate_weights.T
    block = 2 * CAP

    sent, row_hot, grad_hot, row_gate = prep(ids, gates, tokens, cotangent, experts, parts)
    sent = sent.reshape(parts * experts, block, piece)
    got = lax.all_to_all(sent, both, 0, 0, tiled=True)
    got = got.reshape(parts * experts * block, piece)
    tiled = piece % (2 * LANES) == 0 and parts & (parts - 1) == 0
    back, totals = (tiled_middle if tiled else plain_middle)(got, gate, up, down)
    back = lax.all_to_all(back.reshape(parts * experts, block, piece), both, 0, 0, tiled=True)
    back = back.reshape(parts, experts * block, piece)
    output, grad_tokens = finish(row_hot, grad_hot, row_gate, back)
    return (output, grad_tokens) + tuple(total[None] for total in totals)


def solution(mesh):
    rows = P(("dp", "expert"), None)
    held = P("expert", "dp", None)
    return jax.shard_map(
        body,
        mesh=mesh,
        in_specs=(rows, rows, rows, held, held, held, rows),
        out_specs=(rows, rows, held, held, held),
        check_vma=False,
    )
```
